128 devices in a mesh: row: 8 (over z, x_lo), col: 16 (over x_hi, y, core).
Axes of the slice: x: 4 (x_hi: 2, x_lo: 2; x = x_hi * 2 + x_lo), y: 4, z: 4, core: 2. Of those that a mesh axis runs over, the one named last changes fastest.
Arguments:
- front: float32 [62464, 2048], P('row', 'col')
- child_update: bfloat16 [62464, 2048], P('row', 'col'), may hold values from -6 to 6
- child_rows: int32 [4, 244], replicated, may hold values from 16 to 487, as said below
Outputs:
- factor: float32 [62464, 2048], P('row', 'col')
The draws below stay inside these ranges and needn't reach their ends.
Inputs may be any that keep to these rules, and one draw needn't show every extreme that they name: `child_rows`: each row names 244 distinct parent block rows, none below 16. Block row b of child c lies on row group (c // 2) * 4 + b // 61; the 61 block rows of one row group go to the parent row groups (each owning 61 consecutive block rows) in turn, from a drawn first one, so at most 8 of them reach one parent row group.
All inputs are finite; a program needn't handle non-finite values.
Results may differ from the reference program's by a relative error of at most 0.0017.
Values may be sent and summed in bfloat16 or wider, within the bound.
No kernel may reach another device: no remote copies, remote signals or barrier semaphores. Data moves between devices by JAX's collectives and lax.ppermute only.
A program may use at most 128 MiB of HBM per device.

```python
import math
import jax
import jax.numpy as jnp

BLOCK = 128
NF = 62464
CR = 31232
STEPS = 3
WC = 2048
TOPB = 16
NGROUPS = 8
HALFG = 4
ROWB = 61
RBC = 61


def draw_front(key, part):
    key_lower = jax.random.fold_in(key, 11)
    key_points = jax.random.fold_in(key, 12)
    key_flip = jax.random.fold_in(key, 13)
    key_scale = jax.random.fold_in(key, 14)
    side_length = math.sqrt(WC)
    points = jax.random.uniform(key_points, (WC, 2), jnp.float32, 0.0, side_length)
    delta_x = points[:, 0][:, None] - points[:, 0][None, :]
    delta_y = points[:, 1][:, None] - points[:, 1][None, :]
    distance = jnp.sqrt(delta_x * delta_x + delta_y * delta_y)
    kernel = jnp.exp(-distance / 1.5)
    scales = jnp.exp(jax.random.uniform(key_scale, (WC,), jnp.float32, jnp.log(0.8), jnp.log(1.25)))
    sign_flip = jnp.where(jax.random.bernoulli(key_flip, 0.5, (WC,)), 1.0, -1.0).astype(jnp.float32)
    lower_rows = jnp.clip(jax.random.normal(key_lower, (NF - WC, WC), jnp.float32), -6.0, 6.0)
    weight = scales * sign_flip
    top_square = weight[:, None] * kernel * weight[None, :] + 0.5 * jnp.eye(WC, dtype=jnp.float32)
    return jnp.concatenate([top_square, lower_rows], axis=0).astype(jnp.float32)


def draw_child_rows(key, part):
    offsets = jax.random.randint(jax.random.fold_in(key, 1), (4, HALFG), 0, NGROUPS)
    positions = jnp.arange(RBC, dtype=jnp.int32)
    group_ids = jnp.arange(NGROUPS, dtype=jnp.int32)
    results = []
    for child_id in range(4):
        targets = (positions[None, :] + offsets[child_id][:, None]) % NGROUPS
        flat_targets = targets.reshape(-1)
        one_hot = (flat_targets[:, None] == group_ids[None, :]).astype(jnp.int32)
        ranking = jnp.sum((jnp.cumsum(one_hot, axis=0) - one_hot) * one_hot, axis=1)
        tables = []
        for group_id in range(NGROUPS):
            group_key = jax.random.fold_in(jax.random.fold_in(key, 100 + child_id), group_id)
            if group_id == 0:
                choose = TOPB + jax.random.permutation(group_key, ROWB - TOPB)
            else:
                choose = jax.random.permutation(group_key, ROWB)[:ROWB - TOPB]
            tables.append(group_id * ROWB + choose.astype(jnp.int32))
        table_all = jnp.stack(tables)
        results.append(table_all[flat_targets, ranking])
    return jnp.stack(results).astype(jnp.int32)


def block_levels(rng, dims, shards, least, largest):
    def one(axis_at, shards_of):
        draws = jax.random.uniform(jax.random.fold_in(jax.random.fold_in(rng, 6), axis_at), (shards_of,), jnp.float32, least / len(shards), largest / len(shards))
        return jnp.repeat(jnp.exp(draws), dims[axis_at] // shards_of).reshape((-1,) + (1,) * (len(dims) - axis_at - 1))

    gain = one(*shards[0])
    for cut in shards[1:]:
        gain = gain * one(*cut)
    return gain


def gaussian(rng, shape, spread, limit, pieces=(), held_as=jnp.bfloat16):
    loudness = block_levels(rng, shape, pieces, -0.22, 0.18) if pieces else 1.0
    values = jax.random.normal(rng, shape, jnp.float32) * spread * loudness
    return jnp.minimum(jnp.maximum(values, -limit), limit).astype(held_as)


def setup_inputs(seed: int = 0) -> dict:
    key_of = jax.random.split(jax.random.key(seed), 4)
    return {
        "front": draw_front(jax.random.fold_in(key_of[3], 71), 0),
        "child_update": gaussian(key_of[1], (2 * CR, WC), 1.0, 6.0, ((0, 8), (1, 16))),
        "child_rows": draw_child_rows(jax.random.fold_in(key_of[3], 71), 0),
    }


def reference(front, child_update, child_rows):
    half_cols = WC // 2
    assembled = front
    for child_id in range(4):
        row_half = child_id // 2
        col_half = child_id % 2
        block_part = child_update[row_half * CR:(row_half + 1) * CR, col_half * half_cols:(col_half + 1) * half_cols].astype(jnp.float32)
        target_rows = (child_rows[child_id][:, None] * BLOCK + jnp.arange(BLOCK, dtype=jnp.int32)[None, :]).reshape(-1)
        assembled = assembled.at[target_rows, col_half * half_cols:(col_half + 1) * half_cols].add(block_part)
    working = assembled
    row_ids = jnp.arange(NF, dtype=jnp.int32)[:, None]
    factor = jnp.zeros((NF, WC), jnp.float32)
    for panel_step in range(STEPS):
        first_col = panel_step * BLOCK
        corner = working[first_col:first_col + BLOCK, first_col:first_col + BLOCK]
        symmetric = jnp.tril(corner) + jnp.tril(corner, -1).T
        lower_factor = jnp.linalg.cholesky(symmetric)
        solved = jax.scipy.linalg.solve_triangular(lower_factor, working[:, first_col:first_col + BLOCK].T, lower=True).T
        placed = jnp.zeros((NF, BLOCK), jnp.float32).at[first_col:first_col + BLOCK].set(lower_factor)
        panel_cols = jnp.where(row_ids < first_col, 0.0, jnp.where(row_ids < first_col + BLOCK, placed, solved))
        factor = factor.at[:, first_col:first_col + BLOCK].set(panel_cols)
        narrow = panel_cols.astype(jnp.bfloat16)
        if first_col + BLOCK < WC:
            update = jnp.dot(narrow.astype(jnp.float32), narrow[first_col + BLOCK:WC].T.astype(jnp.float32), preferred_element_type=jnp.float32)
            working = working.at[:, first_col + BLOCK:].add(-update)
    rest_cols = STEPS * BLOCK
    if rest_cols < WC:
        factor = factor.at[:, rest_cols:].set(working[:, rest_cols:])
    col_ids = jnp.arange(WC, dtype=jnp.int32)[None, :]
    return jnp.where(row_ids >= col_ids, factor, 0.0)
```

```python
import functools

import jax
import jax.numpy as jnp
from jax import lax
from jax.experimental import pallas as pl
from jax.experimental.pallas import tpu as pltpu
from jax.sharding import PartitionSpec as P


B = 128
STEPS = 3
RB = 61
ROWS = RB * B
NR = 8
NC = 16
TOP = NC
CH = 4
NQ = NC // 2
F32 = jnp.float32
BF16 = jnp.bfloat16
HI = lax.Precision.HIGHEST
VM = pl.BlockSpec(memory_space=pltpu.VMEM)
SM = pl.BlockSpec(memory_space=pltpu.SMEM)
ANY = pl.BlockSpec(memory_space=pl.ANY)


def params(mib=56):
    return pltpu.CompilerParams(vmem_limit_bytes=mib * 1024 * 1024)


def cost(us):
    return pl.CostEstimate(flops=int(us * 9e8), bytes_accessed=int(us * 3e6), transcendentals=0)


def dot_t(a, b, precision=None):
    return lax.dot_general(
        a, b, (((1,), (1,)), ((), ())), precision=precision, preferred_element_type=F32
    )


def chunk_block(owner, t):
    return owner if t == 0 else TOP + 3 * owner + t - 1


def pack_kernel(pos, rows, child, out, sems):
    row, half = pos[0], pos[1] // (NC // 2)
    c, g = 2 * (row // (NR // 2)) + half, row % (NR // 2)
    first = rows[c, g * RB] // RB
    copies = []
    for d in range(NR):
        residue = (d - first + NR) % NR
        for s in range(NR):
            p = jnp.minimum(NR * s + residue, RB - 1)
            copies.append(
                pltpu.make_async_copy(
                    child.at[pl.ds(pl.multiple_of(p * B, B), B)],
                    out.at[pl.ds((d * NR + s) * B, B)],
                    sems.at[d * NR + s],
                )
            )
            copies[-1].start()
    for copy in copies:
        copy.wait()


def pack(pos, rows, child):
    return pl.pallas_call(
        pack_kernel,
        out_shape=jax.ShapeDtypeStruct((NR * NR * B, B), BF16),
        in_specs=[SM, SM, ANY],
        out_specs=VM,
        scratch_shapes=[pltpu.SemaphoreType.DMA((NR * NR,))],
        compiler_params=params(),
        cost_estimate=cost(3),
        name="pack",
    )(pos, rows, child)


def assemble_kernel(pos, rows, front, got, work, *chunks):
    row, col = pos[0], pos[1]
    half = col // (NC // 2)
    work[...] = front[...]
    for src in range(NR):
        c, g = 2 * (src // (NR // 2)) + half, src % (NR // 2)
        first = rows[c, g * RB] // RB
        residue = (row - first + NR) % NR

        def add(s, carry, src=src, c=c, g=g, residue=residue):
            p = NR * s + residue

            @pl.when(p < RB)
            def _():
                b = rows[c, g * RB + jnp.minimum(p, RB - 1)] - row * RB
                at = pl.ds(pl.multiple_of(b * B, B), B)
                piece = got[pl.ds(pl.multiple_of((src * NR + s) * B, B), B)]
                work[at] = work[at] + piece.astype(F32)

            return carry

        lax.fori_loop(0, NR, add, 0)

    @pl.when(col < STEPS)
    def _():
        for s in range(NQ):
            chip = (col // 8 + s // 4) % 2 * 4 + (col // 2 + s) % 4
            for c in range(2):
                for t in range(CH):
                    b = jnp.minimum(chunk_block(2 * chip + c, t), RB - 1)
                    at = (c * CH + t) * B
                    chunks[s][at : at + B] = work[pl.ds(pl.multiple_of(b * B, B), B)]


def assemble(pos, rows, front, got):
    return pl.pallas_call(
        assemble_kernel,
        out_shape=[jax.ShapeDtypeStruct((ROWS, B), F32)]
        + [jax.ShapeDtypeStruct((2 * CH * B, B), F32)] * NQ,
        in_specs=[SM, SM, VM, VM],
        out_specs=[VM] * (NQ + 1),
        compiler_params=params(),
        cost_estimate=cost(6),
        name="assemble",
    )(pos, rows, front, got)


NB = 32
NW = 8


def eliminate(m):
    sub = lax.broadcasted_iota(jnp.int32, (NB, B), 0)
    for lo in range(0, B, NB):
        halves = [m[lo : lo + NB, :B], m[lo : lo + NB, B:]]
        for t in range(0, NB, NW):
            spread = [
                jnp.broadcast_to(halves[0][:, lo + t + i : lo + t + i + 1], (NB, B))
                for i in range(NW)
            ]
            lines = [[h[t + i : t + i + 1] for h in halves] for i in range(NW)]
            for i in range(NW):
                scale = lax.rsqrt(spread[i][t + i : t + i + 1])
                spread[i] = spread[i] * scale
                lines[i] = [line * scale for line in lines[i]]
                for n in range(i + 1, NW):
                    ratio = spread[i][t + n : t + n + 1]
                    spread[n] = spread[n] - spread[i] * ratio
                    lines[n] = [a - ratio * b for a, b in zip(lines[n], lines[i], strict=True)]
            for i in range(NW):
                ratio = jnp.where(sub >= t + NW, spread[i], 0.0)
                halves = [h - ratio * line for h, line in zip(halves, lines[i], strict=True)]
            for i in range(NW):
                halves = [
                    jnp.where(sub == t + i, line, h)
                    for h, line in zip(halves, lines[i], strict=True)
                ]
        r = jnp.concatenate(halves, axis=1)
        m[lo : lo + NB] = r
        if lo + NB < B:
            m[lo + NB :] = m[lo + NB :] - lax.dot_general(
                r[:, lo + NB : B],
                r,
                (((0,), (0,)), ((), ())),
                precision=HI,
                preferred_element_type=F32,
            )


def factor_kernel(top, low, inv, facing, m):
    lane = lax.broadcasted_iota(jnp.int32, (B, B), 1)
    sub = lax.broadcasted_iota(jnp.int32, (B, B), 0)

    def load(a):
        m[:, :B] = jnp.where(sub >= lane, a, a.T)
        m[:, B:] = jnp.where(lane == sub, 1.0, 0.0).astype(F32)

    def part(i):
        return top[i * B : (i + 1) * B]

    load(part(0))

    def step(k, carry):
        eliminate(m)
        low[k] = jnp.where(lane >= sub, m[:, :B], 0.0).T
        inverse = m[:, B:]
        inv[k] = inverse

        @pl.when(k == 0)
        def _():
            n01 = dot_t(part(1), inverse, HI).astype(BF16)
            facing[0] = n01
            facing[1] = dot_t(part(2), inverse, HI).astype(BF16)
            load(part(3) - dot_t(n01, n01))

        @pl.when(k == 1)
        def _():
            n02 = facing[1]
            n12 = dot_t(part(4) - dot_t(n02, facing[0]), inverse, HI).astype(BF16)
            facing[2] = n12
            load(part(5) - dot_t(n02, n02) - dot_t(n12, n12))

        return carry

    lax.fori_loop(0, STEPS, step, 0)


def factor(top):
    return pl.pallas_call(
        factor_kernel,
        out_shape=[
            jax.ShapeDtypeStruct((STEPS, B, B), F32),
            jax.ShapeDtypeStruct((STEPS, B, B), F32),
            jax.ShapeDtypeStruct((STEPS, B, B), BF16),
        ],
        in_specs=[VM],
        out_specs=[VM] * 3,
        scratch_shapes=[pltpu.VMEM((B, 2 * B), F32)],
        compiler_params=params(),
        cost_estimate=cost(15),
        name="factor",
    )(top)


def sort_kernel(pos, *refs):
    pieces, keep, give, held, sems = refs[:NQ], *refs[NQ:]
    col = pos[1]
    x, y, core = col // 8, col // 2 % 4, col % 2
    half = CH * B
    for n, k in ((0, jnp.where(core == 0, 0, 1)), (1, 2)):
        shift = x * 4 + (y - k // 2 + 4) % 4
        for s in range(NQ):

            @pl.when(shift == s)
            def _(n=n, s=s):
                pltpu.make_async_copy(pieces[s], held.at[n], sems.at[n]).start()

    for n in range(2):
        pltpu.make_async_copy(pieces[0], held.at[n], sems.at[n]).wait()
    for n in range(2):
        at = slice(n * half, (n + 1) * half)
        keep[at] = held[n, pl.ds(pl.multiple_of(core * half, half), half)]
        give[at] = held[n, pl.ds(pl.multiple_of((1 - core) * half, half), half)]


def sort(pos, pieces):
    shape = jax.ShapeDtypeStruct((2 * CH * B, B), F32)
    return pl.pallas_call(
        sort_kernel,
        out_shape=[shape, shape],
        in_specs=[SM] + [ANY] * NQ,
        out_specs=[VM, VM],
        scratch_shapes=[
            pltpu.VMEM((2, 2 * CH * B, B), F32),
            pltpu.SemaphoreType.DMA((2,)),
        ],
        compiler_params=params(),
        cost_estimate=cost(2),
        name="sort",
    )(pos, *pieces)


def panels_kernel(pos, inv, facing, keep, got, out):
    first = pos[1] % 2 == 0
    half = CH * B
    w0 = jnp.where(first, keep[:half], got[:half])
    w1 = jnp.where(first, got[:half], keep[:half])
    w2 = jnp.where(first, keep[half:], got[half:])
    n0 = dot_t(w0, inv[0], HI).astype(BF16)
    out[:, :B] = n0
    n1 = dot_t(w1 - dot_t(n0, facing[0]), inv[1], HI).astype(BF16)
    out[:, B : 2 * B] = n1
    rest = w2 - dot_t(n0, facing[1]) - dot_t(n1, facing[2])
    out[:, 2 * B :] = dot_t(rest, inv[2], HI).astype(BF16)


def panels(pos, inv, facing, keep, got):
    return pl.pallas_call(
        panels_kernel,
        out_shape=jax.ShapeDtypeStruct((CH * B, STEPS * B), BF16),
        in_specs=[SM] + [VM] * 4,
        out_specs=VM,
        compiler_params=params(),
        cost_estimate=cost(4),
        name="panels",
    )(pos, inv, facing, keep, got)


def solve_kernel(pos, work, inv, chunk, out):
    del chunk
    col = pos[1]

    @pl.when(col >= STEPS)
    def _():
        out[...] = work[...]

    @pl.when(col < STEPS)
    def _():
        inverse = inv[jnp.minimum(col, STEPS - 1)]

        def solve(b, carry):
            at = pl.ds(pl.multiple_of(b * (ROWS // NR), 8), ROWS // NR)
            out[at] = dot_t(work[at], inverse, HI)
            return carry

        lax.fori_loop(0, NR, solve, 0)


def solve(pos, work, inv, chunk):
    return pl.pallas_call(
        solve_kernel,
        out_shape=jax.ShapeDtypeStruct((ROWS, B), F32),
        in_specs=[SM, VM, VM, ANY],
        out_specs=VM,
        compiler_params=params(),
        cost_estimate=cost(20),
        name="solve",
    )(pos, work, inv, chunk)


def across_kernel(pos, face, inv, parts):
    col = pos[1]
    lane = lax.broadcasted_iota(jnp.int32, (B, STEPS * B), 1) // B
    across = jnp.where(lane < col, face[...].astype(F32), 0.0)
    parts[0] = across.astype(BF16)

    @pl.when(col < STEPS)
    def _():
        inverse = inv[jnp.minimum(col, STEPS - 1)]
        rest = lax.dot_general(
            inverse, across, (((1,), (0,)), ((), ())), precision=HI, preferred_element_type=F32
        )
        for i in range(3):
            parts[i] = rest.astype(BF16)
            rest = rest - parts[i].astype(F32)


def across(pos, face, inv):
    return pl.pallas_call(
        across_kernel,
        out_shape=jax.ShapeDtypeStruct((3, B, STEPS * B), BF16),
        in_specs=[SM, VM, VM],
        out_specs=VM,
        compiler_params=params(),
        cost_estimate=cost(1),
        name="across",
    )(pos, face, inv)


def update_kernel(flip, pos, work, panel, parts, low, out, held, ins, outs):
    row, col = pos[0], pos[1]
    core = (col + flip) % 2

    def each(q, there, act):
        owner = 2 * q + core
        sems = outs if there else ins
        for n, (first, t, end) in enumerate(((owner, 0, 1), (TOP + 3 * owner, 1, CH))):
            hbm = pl.ds(pl.multiple_of(first * B, B), (end - t) * B)
            here = held.at[q, pl.ds(t * B, (end - t) * B)]
            copy = (
                pltpu.make_async_copy(here, out.at[hbm], sems.at[q, n])
                if there
                else pltpu.make_async_copy(work.at[hbm], here, sems.at[q, n])
            )
            if t and q == NQ - 1:
                pl.when(owner < NC - 1)(lambda copy=copy: act(copy))
            else:
                act(copy)

    for q in range(NQ):
        each(q, False, lambda copy: copy.start())
    for q in range(NQ):
        owner = 2 * q + core
        rows = slice(q * CH * B, (q + 1) * CH * B)
        each(q, False, lambda copy: copy.wait())

        @pl.when(col >= STEPS)
        def _(q=q, rows=rows):
            held[q] = held[q] - dot_t(panel[rows], parts[0])

        for k in range(1, STEPS):

            @pl.when(col == k)
            def _(k=k, q=q, rows=rows):
                left = panel[rows, : k * B]
                total = dot_t(left, parts[0, :, : k * B])
                for i in range(1, 3):
                    total = total + dot_t(left, parts[i, :, : k * B])
                held[q] = held[q] - total

        @pl.when((row == 0) & (owner <= col))
        def _(q=q, owner=owner):
            r = lax.broadcasted_iota(jnp.int32, (B, B), 0)
            c = lax.broadcasted_iota(jnp.int32, (B, B), 1)
            value = jnp.where(col < STEPS, low[jnp.minimum(col, STEPS - 1)], held[q, :B])
            held[q, :B] = jnp.where((owner == col) & (r >= c), value, 0.0)

        each(q, True, lambda copy: copy.start())

    for q in range(NQ):
        each(q, True, lambda copy: copy.wait())


def update(flip, pos, work, panel, parts, low):
    return pl.pallas_call(
        functools.partial(update_kernel, flip),
        out_shape=jax.ShapeDtypeStruct((ROWS, B), F32),
        in_specs=[SM, ANY, VM, VM, VM],
        out_specs=ANY,
        input_output_aliases={1: 0},
        scratch_shapes=[
            pltpu.VMEM((NQ, CH * B, B), F32),
            pltpu.SemaphoreType.DMA((NQ, 2)),
            pltpu.SemaphoreType.DMA((NQ, 2)),
        ],
        compiler_params=params(),
        cost_estimate=cost(6),
        name="update",
    )(pos, work, panel, parts, low)


def send(x, pairs):
    return lax.ppermute(x, ("row", "col"), [(a * NC + b, c * NC + d) for (a, b), (c, d) in pairs])


def spread_top(front, row, col):
    parts = [front[k * B : STEPS * B] for k in range(STEPS)]
    second = send(parts[1], [((0, 1), (0, 0))])
    third = send(parts[2], [((0, 2), (0, 0))])
    root = (row == 0) & (col == 0)
    top = jnp.where(root, jnp.concatenate([parts[0], second, third]), 0.0)

    def hop(top, *moves):
        return sum([send(top, pairs) for pairs in moves], top)

    even = range(0, NC, 2)
    targets = (2, 6, 8, 4)
    top = hop(top, *[[((0, 0), (0, c))] for c in targets])
    top = hop(top, [((0, c), (0, c + 8)) for c in (2, 4, 6)])
    top = hop(top, [((0, c), (1, c)) for c in even])
    pair = [(r, c) for r in range(2) for c in even]
    top = hop(top, [((r, c), (r + 2, c)) for r, c in pair], [((r, c), (r + 6, c)) for r, c in pair])
    top = hop(top, [((r + 2, c), (r + 4, c)) for r, c in pair])
    return hop(top, [((r, c), (r, c + 1)) for c in even for r in range(NR)])


def on_device(front, child_update, child_rows):
    row, col = lax.axis_index("row"), lax.axis_index("col")
    pos = jnp.stack([row, col]).astype(jnp.int32)
    packed = pack(pos, child_rows, child_update)
    got = lax.all_to_all(packed, "row", 0, 0, tiled=True)
    top = spread_top(front, row, col)
    low, inv, facing = factor(top)
    work, *chunks = assemble(pos, child_rows, front, got)

    def outward(s):
        pairs = []
        for k in range(STEPS):
            pairs.append((k, s // 4 * 8 + (k // 2 + s) % 4 * 2 + k % 2))
        return lax.ppermute(chunks[s], "col", pairs)

    def home(k, dx, dy):
        return dx * 8 + (k // 2 + dy) % 4 * 2 + k % 2

    pieces = {0: chunks[0]}
    relayed = lax.ppermute(chunks[7], "col", [(k, home(k, 0, 3)) for k in range(STEPS)])
    order = (1, 4, 2, 5, 3, 6)
    for s in order:
        pieces[s] = outward(s)
    pieces[7] = lax.ppermute(relayed, "col", [(home(k, 0, 3), home(k, 1, 3)) for k in range(STEPS)])
    keep, give = sort(pos, [pieces[s] for s in range(NQ)])
    flip = [(c, c ^ 1) for c in range(NC)]
    chunk = panels(pos, inv, facing, keep, lax.ppermute(give, "col", flip))
    cores = [[c for c in range(NC) if c % 2 == p] for p in range(2)]
    mine = lax.all_to_all(
        jnp.tile(chunk, (NQ, 1)), "col", 0, 0, axis_index_groups=cores, tiled=True
    )
    face = jnp.where(row == 0, chunk[:B], jnp.zeros_like(chunk[:B]))

    def hop(face, *moves):
        return sum([lax.ppermute(face, "row", pairs) for pairs in moves], face)

    face = hop(face, [(0, 2)], [(0, 6)])
    face = hop(face, [(2, 4)])
    face = hop(face, [(0, 1), (2, 3), (4, 5), (6, 7)])
    parts = across(pos, face, inv)
    work = solve(pos, work, inv, chunk)
    work = update(0, pos, work, mine, parts, low)
    other = lax.ppermute(mine, "col", flip)
    return update(1, pos, work, other, parts, low)


def solution(mesh):
    in_specs = (P("row", "col"), P("row", "col"), P())
    return jax.shard_map(
        on_device, mesh=mesh, in_specs=in_specs, out_specs=P("row", "col"), check_vma=False
    )
```

```python
import functools

import jax
import jax.numpy as jnp
from jax import lax
from jax.experimental import pallas as pl
from jax.experimental.pallas import tpu as pltpu
from jax.sharding import PartitionSpec as P


B = 128
STEPS = 3
RB = 61
ROWS = RB * B
NR = 8
NC = 16
TOP = NC
CH = 4
NQ = NC // 2
SPLIT = 5
F32 = jnp.float32
BF16 = jnp.bfloat16
HI = lax.Precision.HIGHEST
VM = pl.BlockSpec(memory_space=pltpu.VMEM)
SM = pl.BlockSpec(memory_space=pltpu.SMEM)
ANY = pl.BlockSpec(memory_space=pl.ANY)


def params(mib):
    return pltpu.CompilerParams(vmem_limit_bytes=mib * 1024 * 1024)


def cost(us):
    return pl.CostEstimate(flops=int(us * 9e8), bytes_accessed=int(us * 3e6), transcendentals=0)


def dot_t(a, b, precision=None):
    return lax.dot_general(
        a, b, (((1,), (1,)), ((), ())), precision=precision, preferred_element_type=F32
    )


def pack_kernel(pos, rows, child, out, sems):
    row, half = pos[0], pos[1] // (NC // 2)
    c, g = 2 * (row // (NR // 2)) + half, row % (NR // 2)
    first = rows[c, g * RB] // RB
    copies = []
    for d in range(NR):
        residue = (d - first + NR) % NR
        for s in range(NR):
            p = jnp.minimum(NR * s + residue, RB - 1)
            copies.append(
                pltpu.make_async_copy(
                    child.at[pl.ds(pl.multiple_of(p * B, B), B)],
                    out.at[pl.ds((d * NR + s) * B, B)],
                    sems.at[d * NR + s],
                )
            )
            copies[-1].start()
    for copy in copies:
        copy.wait()


def pack(pos, rows, child):
    return pl.pallas_call(
        pack_kernel,
        out_shape=jax.ShapeDtypeStruct((NR * NR * B, B), BF16),
        in_specs=[SM, SM, ANY],
        out_specs=VM,
        scratch_shapes=[pltpu.SemaphoreType.DMA((NR * NR,))],
        compiler_params=params(56),
        cost_estimate=cost(3),
        name="pack",
    )(pos, rows, child)


def assemble_kernel(pos, rows, front, got, work, *refs):
    chunks, (slab, child, load, arrive, store, send) = refs[: NQ + 1], refs[NQ + 1 :]
    row, col = pos[0], pos[1]
    half = col // (NC // 2)
    part, group = ROWS // NR, NR * B

    def pieces(there):
        for i in range(NR):
            at = pl.ds(i * part, part)
            if there:
                yield pltpu.make_async_copy(slab.at[at], work.at[at], store.at[i])
            else:
                yield pltpu.make_async_copy(front.at[at], slab.at[at], load.at[i])

    arrivals = [
        pltpu.make_async_copy(
            got.at[pl.ds(i * group, group)], child.at[pl.ds(i * group, group)], arrive.at[i]
        )
        for i in range(NR)
    ]
    for copy in pieces(False):
        copy.start()
    for copy in arrivals:
        copy.start()
    for copy in pieces(False):
        copy.wait()
    for src in range(NR):
        arrivals[src].wait()
        c, g = 2 * (src // (NR // 2)) + half, src % (NR // 2)
        first = rows[c, g * RB] // RB
        residue = (row - first + NR) % NR

        def add(s, src=src, c=c, g=g, residue=residue):
            p = NR * s + residue
            b = rows[c, g * RB + jnp.minimum(p, RB - 1)] - row * RB
            at = pl.ds(pl.multiple_of(b * B, B), B)
            start = (src * NR + s) * B
            slab[at] = slab[at] + child[start : start + B].astype(F32)

        for s in range(NR - 1):
            add(s)
        pl.when(NR * (NR - 1) + residue < RB)(functools.partial(add, NR - 1))

    def messages():
        for s in range(NQ):
            chip = (col // 8 + s // 4) % 2 * 4 + (col // 2 + s) % 4
            for c in range(2):
                owner = 2 * chip + c
                body = jnp.minimum(TOP + 3 * owner, RB - 3)
                target, base = (chunks[s], c * CH) if s != SPLIT else (chunks[s + c * (NQ - s)], 0)
                for n, (b, t, end) in enumerate(((owner, 0, 1), (body, 1, CH))):
                    yield pltpu.make_async_copy(
                        slab.at[pl.ds(pl.multiple_of(b * B, B), (end - t) * B)],
                        target.at[pl.ds((base + t) * B, (end - t) * B)],
                        send.at[s, c, n],
                    )

    @pl.when(col < STEPS)
    def _():
        for copy in messages():
            copy.start()

    for copy in pieces(True):
        copy.start()

    @pl.when(col < STEPS)
    def _():
        for copy in messages():
            copy.wait()

    for copy in pieces(True):
        copy.wait()


def assemble(pos, rows, front, got):
    return pl.pallas_call(
        assemble_kernel,
        out_shape=[jax.ShapeDtypeStruct((ROWS, B), F32)]
        + [jax.ShapeDtypeStruct(((1 + (s not in (SPLIT, NQ))) * CH * B, B), F32) for s in range(NQ + 1)],
        in_specs=[SM, SM, ANY, ANY],
        out_specs=[ANY] * (NQ + 2),
        scratch_shapes=[
            pltpu.VMEM((ROWS, B), F32),
            pltpu.VMEM((NR * NR * B, B), BF16),
            pltpu.SemaphoreType.DMA((NR,)),
            pltpu.SemaphoreType.DMA((NR,)),
            pltpu.SemaphoreType.DMA((NR,)),
            pltpu.SemaphoreType.DMA((NQ, 2, 2)),
        ],
        compiler_params=params(61),
        cost_estimate=cost(6),
        name="assemble",
    )(pos, rows, front, got)


NB = 32
NW = 8


def eliminate(m):
    sub = lax.broadcasted_iota(jnp.int32, (NB, B), 0)
    for lo in range(0, B, NB):
        halves = [m[lo : lo + NB, :B], m[lo : lo + NB, B:]]
        for t in range(0, NB, NW):
            spread = [
                jnp.broadcast_to(halves[0][:, lo + t + i : lo + t + i + 1], (NB, B))
                for i in range(NW)
            ]
            lines = [[h[t + i : t + i + 1] for h in halves] for i in range(NW)]
            for i in range(NW):
                scale = lax.rsqrt(spread[i][t + i : t + i + 1])
                spread[i] = spread[i] * scale
                lines[i] = [line * scale for line in lines[i]]
                for n in range(i + 1, NW):
                    ratio = spread[i][t + n : t + n + 1]
                    spread[n] = spread[n] - spread[i] * ratio
                    lines[n] = [a - ratio * b for a, b in zip(lines[n], lines[i], strict=True)]
            for i in range(NW):
                ratio = jnp.where(sub >= t + NW, spread[i], 0.0)
                halves = [h - ratio * line for h, line in zip(halves, lines[i], strict=True)]
            for i in range(NW):
                halves = [
                    jnp.where(sub == t + i, line, h)
                    for h, line in zip(halves, lines[i], strict=True)
                ]
        r = jnp.concatenate(halves, axis=1)
        m[lo : lo + NB] = r
        if lo + NB < B:
            m[lo + NB :] = m[lo + NB :] - lax.dot_general(
                r[:, lo + NB : B],
                r,
                (((0,), (0,)), ((), ())),
                precision=HI,
                preferred_element_type=F32,
            )


def factor_kernel(top, low, inv, facing, m):
    lane = lax.broadcasted_iota(jnp.int32, (B, B), 1)
    sub = lax.broadcasted_iota(jnp.int32, (B, B), 0)

    def load(a):
        m[:, :B] = jnp.where(sub >= lane, a, a.T)
        m[:, B:] = jnp.where(lane == sub, 1.0, 0.0).astype(F32)

    def part(i):
        return top[i * B : (i + 1) * B]

    load(part(0))

    def step(k, carry):
        eliminate(m)
        low[k] = jnp.where(lane >= sub, m[:, :B], 0.0).T
        inverse = m[:, B:]
        inv[k] = inverse

        @pl.when(k == 0)
        def _():
            n01 = dot_t(part(1), inverse, HI).astype(BF16)
            facing[0] = n01
            facing[1] = dot_t(part(2), inverse, HI).astype(BF16)
            load(part(3) - dot_t(n01, n01))

        @pl.when(k == 1)
        def _():
            n02 = facing[1]
            n12 = dot_t(part(4) - dot_t(n02, facing[0]), inverse, HI).astype(BF16)
            facing[2] = n12
            load(part(5) - dot_t(n02, n02) - dot_t(n12, n12))

        return carry

    lax.fori_loop(0, STEPS, step, 0)


def factor(top):
    return pl.pallas_call(
        factor_kernel,
        out_shape=[
            jax.ShapeDtypeStruct((STEPS, B, B), F32),
            jax.ShapeDtypeStruct((STEPS, B, B), F32),
            jax.ShapeDtypeStruct((STEPS, B, B), BF16),
        ],
        in_specs=[VM],
        out_specs=[VM] * 3,
        scratch_shapes=[pltpu.VMEM((B, 2 * B), F32)],
        compiler_params=params(5),
        cost_estimate=cost(15),
        name="factor",
    )(top)


def sort_kernel(pos, *refs):
    pieces, (other, direct, keep, give, sems) = refs[:NQ], refs[NQ:]
    col = pos[1]
    x, y, core = col // 8, col // 2 % 4, col % 2
    half = CH * B

    def copies(n, sources):
        for i, (out, source) in enumerate(zip((keep, give), sources, strict=True)):
            yield pltpu.make_async_copy(source, out.at[pl.ds(n * half, half)], sems.at[n, i])

    def sides(piece):
        return [
            piece.at[pl.ds(pl.multiple_of(side * half, half), half)] for side in (core, 1 - core)
        ]

    def start(n, sources):
        for copy in copies(n, sources):
            copy.start()

    for n, k in ((0, jnp.where(core == 0, 0, 1)), (1, 2)):
        shift = x * 4 + (y - k // 2 + 4) % 4
        for s in range(NQ):
            if s == SPLIT:
                two = [pieces[s], other]
                pl.when((shift == s) & (core == 0))(functools.partial(start, n, two))
                pl.when((shift == s) & (core == 1))(functools.partial(start, n, two[::-1]))
            else:
                piece = direct if (n, s) == (1, NQ - 1) else pieces[s]
                pl.when(shift == s)(functools.partial(start, n, sides(piece)))

    for n in range(2):
        for copy in copies(n, sides(pieces[0])):
            copy.wait()


def sort(pos, pieces):
    shape = jax.ShapeDtypeStruct((2 * CH * B, B), F32)
    return pl.pallas_call(
        sort_kernel,
        out_shape=[shape, shape],
        in_specs=[SM] + [ANY] * (NQ + 2),
        out_specs=[VM, VM],
        scratch_shapes=[pltpu.SemaphoreType.DMA((2, 2))],
        compiler_params=params(4),
        cost_estimate=cost(2),
        name="sort",
    )(pos, *pieces)


def panels_kernel(pos, inv, facing, keep, got, out, held, chunk, load, store):
    core = pos[1] % 2
    half = CH * B
    lower, upper = pl.ds(0, half), pl.ds(half, half)

    def copies(sources):
        for k, (ref, at) in enumerate(sources):
            yield pltpu.make_async_copy(ref.at[at], held.at[k], load.at[k])

    even = ((keep, lower), (got, lower), (keep, upper))
    odd = ((got, lower), (keep, lower), (got, upper))

    @pl.when(core == 0)
    def _():
        for copy in copies(even):
            copy.start()

    @pl.when(core == 1)
    def _():
        for copy in copies(odd):
            copy.start()

    waits = list(copies(even))
    waits[0].wait()
    n0 = dot_t(held[0], inv[0], HI).astype(BF16)
    chunk[:, :B] = n0
    waits[1].wait()
    n1 = dot_t(held[1] - dot_t(n0, facing[0]), inv[1], HI).astype(BF16)
    chunk[:, B : 2 * B] = n1
    waits[2].wait()
    rest = held[2] - dot_t(n0, facing[1]) - dot_t(n1, facing[2])
    chunk[:, 2 * B :] = dot_t(rest, inv[2], HI).astype(BF16)
    stores = [
        pltpu.make_async_copy(chunk, out.at[pl.ds(q * half, half)], store.at[q]) for q in range(NQ)
    ]
    for copy in stores:
        copy.start()
    for copy in stores:
        copy.wait()


def panels(pos, inv, facing, keep, got):
    return pl.pallas_call(
        panels_kernel,
        out_shape=jax.ShapeDtypeStruct((NQ * CH * B, STEPS * B), BF16),
        in_specs=[SM, VM, VM, ANY, ANY],
        out_specs=ANY,
        scratch_shapes=[
            pltpu.VMEM((STEPS, CH * B, B), F32),
            pltpu.VMEM((CH * B, STEPS * B), BF16),
            pltpu.SemaphoreType.DMA((STEPS,)),
            pltpu.SemaphoreType.DMA((NQ,)),
        ],
        compiler_params=params(6),
        cost_estimate=cost(4),
        name="panels",
    )(pos, inv, facing, keep, got)


def solve_kernel(pos, work, inv, chunk, out):
    del chunk
    col = pos[1]

    @pl.when(col >= STEPS)
    def _():
        out[...] = work[...]

    @pl.when(col < STEPS)
    def _():
        inverse = inv[jnp.minimum(col, STEPS - 1)]

        def solve(b, carry):
            at = pl.ds(pl.multiple_of(b * (ROWS // NR), 8), ROWS // NR)
            out[at] = dot_t(work[at], inverse, HI)
            return carry

        lax.fori_loop(0, NR, solve, 0)


def solve(pos, work, inv, chunk):
    return pl.pallas_call(
        solve_kernel,
        out_shape=jax.ShapeDtypeStruct((ROWS, B), F32),
        in_specs=[SM, VM, VM, ANY],
        out_specs=VM,
        compiler_params=params(12),
        cost_estimate=cost(20),
        name="solve",
    )(pos, work, inv, chunk)


def across_kernel(pos, face, inv, parts):
    col = pos[1]
    lane = lax.broadcasted_iota(jnp.int32, (B, STEPS * B), 1) // B
    across = jnp.where(lane < col, face[...].astype(F32), 0.0)
    parts[0] = across.astype(BF16)

    @pl.when(col < STEPS)
    def _():
        inverse = inv[jnp.minimum(col, STEPS - 1)]
        rest = lax.dot_general(
            inverse, across, (((1,), (0,)), ((), ())), precision=HI, preferred_element_type=F32
        )
        for i in range(3):
            parts[i] = rest.astype(BF16)
            rest = rest - parts[i].astype(F32)


def across(pos, face, inv):
    return pl.pallas_call(
        across_kernel,
        out_shape=jax.ShapeDtypeStruct((3, B, STEPS * B), BF16),
        in_specs=[SM, VM, VM],
        out_specs=VM,
        compiler_params=params(3),
        cost_estimate=cost(1),
        name="across",
    )(pos, face, inv)


def update_kernel(flip, pos, work, narrow, parts, low, out, held, panel, ins, outs, reads):
    row, col = pos[0], pos[1]
    size = CH * B
    loads = [
        pltpu.make_async_copy(
            narrow.at[pl.ds(q * size, size)], panel.at[pl.ds(q * size, size)], reads.at[q]
        )
        for q in range(NQ)
    ]
    core = (col + flip) % 2

    def each(q, there, act):
        owner = 2 * q + core
        sems = outs if there else ins
        for n, (first, t, end) in enumerate(((owner, 0, 1), (TOP + 3 * owner, 1, CH))):
            hbm = pl.ds(pl.multiple_of(first * B, B), (end - t) * B)
            here = held.at[q, pl.ds(t * B, (end - t) * B)]
            copy = (
                pltpu.make_async_copy(here, out.at[hbm], sems.at[q, n])
                if there
                else pltpu.make_async_copy(work.at[hbm], here, sems.at[q, n])
            )
            if t and q == NQ - 1:
                pl.when(owner < NC - 1)(lambda copy=copy: act(copy))
            else:
                act(copy)

    for q in range(NQ):
        loads[q].start()
        each(q, False, lambda copy: copy.start())
    for q in range(NQ):
        owner = 2 * q + core
        rows = slice(q * size, (q + 1) * size)
        loads[q].wait()
        each(q, False, lambda copy: copy.wait())

        @pl.when(col >= STEPS)
        def _(q=q, rows=rows):
            held[q] = held[q] - dot_t(panel[rows], parts[0])

        for k in range(1, STEPS):

            @pl.when(col == k)
            def _(k=k, q=q, rows=rows):
                left = panel[rows, : k * B]
                total = dot_t(left, parts[0, :, : k * B])
                for i in range(1, 3):
                    total = total + dot_t(left, parts[i, :, : k * B])
                held[q] = held[q] - total

        @pl.when((row == 0) & (owner <= col))
        def _(q=q, owner=owner):
            r = lax.broadcasted_iota(jnp.int32, (B, B), 0)
            c = lax.broadcasted_iota(jnp.int32, (B, B), 1)
            value = jnp.where(col < STEPS, low[jnp.minimum(col, STEPS - 1)], held[q, :B])
            held[q, :B] = jnp.where((owner == col) & (r >= c), value, 0.0)

        each(q, True, lambda copy: copy.start())

    for q in range(NQ):
        each(q, True, lambda copy: copy.wait())


def update(flip, pos, work, panel, parts, low):
    return pl.pallas_call(
        functools.partial(update_kernel, flip),
        out_shape=jax.ShapeDtypeStruct((ROWS, B), F32),
        in_specs=[SM, ANY, ANY, VM, VM],
        out_specs=ANY,
        input_output_aliases={1: 0},
        scratch_shapes=[
            pltpu.VMEM((NQ, CH * B, B), F32),
            pltpu.VMEM((NQ * CH * B, STEPS * B), BF16),
            pltpu.SemaphoreType.DMA((NQ, 2)),
            pltpu.SemaphoreType.DMA((NQ, 2)),
            pltpu.SemaphoreType.DMA((NQ,)),
        ],
        compiler_params=params(8),
        cost_estimate=cost(6),
        name="update",
    )(pos, work, panel, parts, low)


def send(x, pairs):
    return lax.ppermute(x, ("row", "col"), [(a * NC + b, c * NC + d) for (a, b), (c, d) in pairs])


def spread_top(front, row, col):
    part = front[: STEPS * B]
    a = send(part, [((0, 0), (0, 2)), ((0, 1), (0, 0)), ((0, 2), (0, 4))])
    b = send(part, [((0, 0), (0, 4)), ((0, 1), (0, 2)), ((0, 2), (0, 6))])
    c = send(part, [((0, 0), (0, 6)), ((0, 1), (0, 4)), ((0, 2), (0, 0))])
    d = send(part, [((0, 1), (0, 6))])

    def pick(at0, at2, at4, at6):
        return jnp.where(col == 0, at0, jnp.where(col == 2, at2, jnp.where(col == 4, at4, at6)))

    columns = [pick(part, a, b, c), pick(a, b, c, d), pick(c, part, a, b)]
    rooted = (row == 0) & (col < NC // 2) & (col % 2 == 0)
    top = jnp.concatenate([v[k * B :] for k, v in enumerate(columns)])
    top = jnp.where(rooted, top, 0.0)

    def hop(top, *moves):
        return sum([send(top, pairs) for pairs in moves], top)

    near = (0, 2, 4, 6)
    beside = [[((0, c), (dr, c + dc)) for c in near] for dr, dc in ((0, 8), (1, 0), (1, 8))]
    top = hop(top, *beside)
    even = range(0, NC, 2)
    away = [[((r, c), (r + dr, c)) for r in range(2) for c in even] for dr in (4, 2, 6)]
    top = hop(top, *away)
    return hop(top, [((r, c), (r, c + 1)) for c in even for r in range(NR)])


def on_device(front, child_update, child_rows):
    row, col = lax.axis_index("row"), lax.axis_index("col")
    pos = jnp.stack([row, col]).astype(jnp.int32)
    packed = pack(pos, child_rows, child_update)
    got = lax.all_to_all(packed, "row", 0, 0, tiled=True)
    top = spread_top(front, row, col)
    low, inv, facing = factor(top)
    work, *chunks = assemble(pos, child_rows, front, got)

    def home(k, dx, dy):
        return dx * 8 + (k // 2 + dy) % 4 * 2 + k % 2

    def step(v, start, end, ks=range(STEPS)):
        return lax.ppermute(v, "col", [(home(k, *start), home(k, *end)) for k in ks])

    pieces = {0: chunks[0]}
    pairs = [(k, home(k, 0, 3)) for k in range(2)] + [(2, home(2, 1, 3))]
    relayed = lax.ppermute(chunks[7], "col", pairs)
    other = step(chunks[NQ], (0, 0), (0, 1))
    for s in (4, 1, 5, 3, 6, 2):
        pieces[s] = step(chunks[s], (0, 0), (s // 4, s % 4))
    pieces[7] = step(relayed, (0, 3), (1, 3), range(2))
    other = step(other, (0, 1), (1, 1))
    keep, give = sort(pos, [pieces[s] for s in range(NQ)] + [other, relayed])
    flip = [(c, c ^ 1) for c in range(NC)]
    chunk = panels(pos, inv, facing, keep, lax.ppermute(give, "col", flip))
    cores = [[c for c in range(NC) if c % 2 == p] for p in range(2)]
    mine = lax.all_to_all(
        chunk, "col", 0, 0, axis_index_groups=cores, tiled=True
    )
    face = jnp.where(row == 0, chunk[:B], jnp.zeros_like(chunk[:B]))

    def hop(face, *moves):
        return sum([lax.ppermute(face, "row", pairs) for pairs in moves], face)

    face = hop(face, [(0, 2)], [(0, 6)])
    face = hop(face, [(2, 4)])
    face = hop(face, [(0, 1), (2, 3), (4, 5), (6, 7)])
    parts = across(pos, face, inv)
    work = solve(pos, work, inv, chunk)
    work = update(0, pos, work, mine, parts, low)
    other = lax.ppermute(mine, "col", flip)
    return update(1, pos, work, other, parts, low)


def solution(mesh):
    in_specs = (P("row", "col"), P("row", "col"), P())
    return jax.shard_map(
        on_device, mesh=mesh, in_specs=in_specs, out_specs=P("row", "col"), check_vma=False
    )
```

```python
import functools

import jax
import jax.numpy as jnp
from jax import lax
from jax.experimental import pallas as pl
from jax.experimental.pallas import tpu as pltpu
from jax.sharding import PartitionSpec as P


B = 128
STEPS = 3
RB = 61
ROWS = RB * B
NR = 8
NC = 16
TOP = NC
CH = 4
NQ = NC // 2
SPLIT = 5
F32 = jnp.float32
BF16 = jnp.bfloat16
HI = lax.Precision.HIGHEST
VM = pl.BlockSpec(memory_space=pltpu.VMEM)
SM = pl.BlockSpec(memory_space=pltpu.SMEM)
ANY = pl.BlockSpec(memory_space=pl.ANY)


def params(mib):
    return pltpu.CompilerParams(vmem_limit_bytes=int(mib * 1024 * 1024))


def cost(us):
    return pl.CostEstimate(flops=int(us * 9e8), bytes_accessed=int(us * 3e6), transcendentals=0)


def dot_t(a, b, precision=None):
    return lax.dot_general(
        a, b, (((1,), (1,)), ((), ())), precision=precision, preferred_element_type=F32
    )


def pack_kernel(pos, rows, child, out, sems):
    row, half = pos[0], pos[1] // (NC // 2)
    c, g = 2 * (row // (NR // 2)) + half, row % (NR // 2)
    first = rows[c, g * RB] // RB
    copies = []
    for d in range(NR):
        residue = (d - first + NR) % NR
        for s in range(NR):
            p = jnp.minimum(NR * s + residue, RB - 1)
            copies.append(
                pltpu.make_async_copy(
                    child.at[pl.ds(pl.multiple_of(p * B, B), B)],
                    out.at[pl.ds((d * NR + s) * B, B)],
                    sems.at[d * NR + s],
                )
            )
            copies[-1].start()
    for copy in copies:
        copy.wait()


def pack(pos, rows, child):
    return pl.pallas_call(
        pack_kernel,
        out_shape=jax.ShapeDtypeStruct((NR * NR * B, B), BF16),
        in_specs=[SM, SM, ANY],
        out_specs=VM,
        scratch_shapes=[pltpu.SemaphoreType.DMA((NR * NR,))],
        compiler_params=params(56),
        cost_estimate=cost(3),
        name="pack",
    )(pos, rows, child)


def assemble_kernel(pos, rows, front, got, work, *refs):
    chunks, (slab, child, load, arrive, store, send) = refs[: NQ + 1], refs[NQ + 1 :]
    row, col = pos[0], pos[1]
    half = col // (NC // 2)
    part, group = ROWS // NR, NR * B

    def pieces(there):
        for i in range(NR):
            at = pl.ds(i * part, part)
            if there:
                yield pltpu.make_async_copy(slab.at[at], work.at[at], store.at[i])
            else:
                yield pltpu.make_async_copy(front.at[at], slab.at[at], load.at[i])

    arrivals = [
        pltpu.make_async_copy(
            got.at[pl.ds(i * group, group)], child.at[pl.ds(i * group, group)], arrive.at[i]
        )
        for i in range(NR)
    ]
    for copy in pieces(False):
        copy.start()
    for copy in arrivals:
        copy.start()
    for copy in pieces(False):
        copy.wait()
    for src in range(NR):
        arrivals[src].wait()
        c, g = 2 * (src // (NR // 2)) + half, src % (NR // 2)
        first = rows[c, g * RB] // RB
        residue = (row - first + NR) % NR

        def add(s, src=src, c=c, g=g, residue=residue):
            p = NR * s + residue
            b = rows[c, g * RB + jnp.minimum(p, RB - 1)] - row * RB
            at = pl.ds(pl.multiple_of(b * B, B), B)
            start = (src * NR + s) * B
            slab[at] = slab[at] + child[start : start + B].astype(F32)

        for s in range(NR - 1):
            add(s)
        pl.when(NR * (NR - 1) + residue < RB)(functools.partial(add, NR - 1))

    def messages():
        for s in range(NQ):
            chip = (col // 8 + s // 4) % 2 * 4 + (col // 2 + s) % 4
            for c in range(2):
                owner = 2 * chip + c
                body = jnp.minimum(TOP + 3 * owner, RB - 3)
                target, base = (chunks[s], c * CH) if s != SPLIT else (chunks[s + c * (NQ - s)], 0)
                for n, (b, t, end) in enumerate(((owner, 0, 1), (body, 1, CH))):
                    yield pltpu.make_async_copy(
                        slab.at[pl.ds(pl.multiple_of(b * B, B), (end - t) * B)],
                        target.at[pl.ds((base + t) * B, (end - t) * B)],
                        send.at[s, c, n],
                    )

    @pl.when(col < STEPS)
    def _():
        for copy in messages():
            copy.start()

    for copy in pieces(True):
        copy.start()

    @pl.when(col < STEPS)
    def _():
        for copy in messages():
            copy.wait()

    for copy in pieces(True):
        copy.wait()


def assemble(pos, rows, front, got):
    return pl.pallas_call(
        assemble_kernel,
        out_shape=[jax.ShapeDtypeStruct((ROWS, B), F32)]
        + [jax.ShapeDtypeStruct(((1 + (s not in (SPLIT, NQ))) * CH * B, B), F32) for s in range(NQ + 1)],
        in_specs=[SM, SM, ANY, ANY],
        out_specs=[ANY] * (NQ + 2),
        scratch_shapes=[
            pltpu.VMEM((ROWS, B), F32),
            pltpu.VMEM((NR * NR * B, B), BF16),
            pltpu.SemaphoreType.DMA((NR,)),
            pltpu.SemaphoreType.DMA((NR,)),
            pltpu.SemaphoreType.DMA((NR,)),
            pltpu.SemaphoreType.DMA((NQ, 2, 2)),
        ],
        compiler_params=params(61),
        cost_estimate=cost(6),
        name="assemble",
    )(pos, rows, front, got)


NB = 64
NW = 16


def eliminate(m):
    sub = lax.broadcasted_iota(jnp.int32, (NB, B), 0)
    for lo in range(0, B, NB):
        halves = [m[lo : lo + NB, :B], m[lo : lo + NB, B:]]
        for t in range(0, NB, NW):
            spread = [
                jnp.broadcast_to(halves[0][:, lo + t + i : lo + t + i + 1], (NB, B))
                for i in range(NW)
            ]
            lines = [[h[t + i : t + i + 1] for h in halves] for i in range(NW)]
            for i in range(NW):
                scale = lax.rsqrt(spread[i][t + i : t + i + 1])
                spread[i] = spread[i] * scale
                lines[i] = [line * scale for line in lines[i]]
                for n in range(i + 1, NW):
                    ratio = spread[i][t + n : t + n + 1]
                    spread[n] = spread[n] - spread[i] * ratio
                    lines[n] = [a - ratio * b for a, b in zip(lines[n], lines[i], strict=True)]
            for i in range(NW):
                ratio = jnp.where(sub >= t + NW, spread[i], 0.0)
                halves = [h - ratio * line for h, line in zip(halves, lines[i], strict=True)]
            for i in range(NW):
                halves = [
                    jnp.where(sub == t + i, line, h)
                    for h, line in zip(halves, lines[i], strict=True)
                ]
        r = jnp.concatenate(halves, axis=1)
        m[lo : lo + NB] = r
        if lo + NB < B:
            m[lo + NB :] = m[lo + NB :] - lax.dot_general(
                r[:, lo + NB : B],
                r,
                (((0,), (0,)), ((), ())),
                precision=HI,
                preferred_element_type=F32,
            )


def factor_kernel(top, low, inv, facing, m):
    lane = lax.broadcasted_iota(jnp.int32, (B, B), 1)
    sub = lax.broadcasted_iota(jnp.int32, (B, B), 0)

    def load(a):
        m[:, :B] = jnp.where(sub >= lane, a, a.T)
        m[:, B:] = jnp.where(lane == sub, 1.0, 0.0).astype(F32)

    def part(i):
        return top[i * B : (i + 1) * B]

    load(part(0))

    def step(k, carry):
        eliminate(m)
        low[k] = jnp.where(lane >= sub, m[:, :B], 0.0).T
        inverse = m[:, B:]
        inv[k] = inverse

        @pl.when(k == 0)
        def _():
            n01 = dot_t(part(1), inverse, HI).astype(BF16)
            facing[0] = n01
            facing[1] = dot_t(part(2), inverse, HI).astype(BF16)
            load(part(3) - dot_t(n01, n01))

        @pl.when(k == 1)
        def _():
            n02 = facing[1]
            n12 = dot_t(part(4) - dot_t(n02, facing[0]), inverse, HI).astype(BF16)
            facing[2] = n12
            load(part(5) - dot_t(n02, n02) - dot_t(n12, n12))

        return carry

    lax.fori_loop(0, STEPS, step, 0)


def factor(top):
    return pl.pallas_call(
        factor_kernel,
        out_shape=[
            jax.ShapeDtypeStruct((STEPS, B, B), F32),
            jax.ShapeDtypeStruct((STEPS, B, B), F32),
            jax.ShapeDtypeStruct((STEPS, B, B), BF16),
        ],
        in_specs=[VM],
        out_specs=[VM] * 3,
        scratch_shapes=[pltpu.VMEM((B, 2 * B), F32)],
        compiler_params=params(5),
        cost_estimate=cost(15),
        name="factor",
    )(top)


def sort_kernel(pos, *refs):
    pieces, (other, direct, keep, give, sems) = refs[:NQ], refs[NQ:]
    col = pos[1]
    x, y, core = col // 8, col // 2 % 4, col % 2
    half = CH * B

    def copies(n, sources):
        for i, (out, source) in enumerate(zip((keep, give), sources, strict=True)):
            yield pltpu.make_async_copy(source, out.at[pl.ds(n * half, half)], sems.at[n, i])

    def sides(piece):
        return [
            piece.at[pl.ds(pl.multiple_of(side * half, half), half)] for side in (core, 1 - core)
        ]

    def start(n, sources):
        for copy in copies(n, sources):
            copy.start()

    for n, k in ((0, jnp.where(core == 0, 0, 1)), (1, 2)):
        shift = x * 4 + (y - k // 2 + 4) % 4
        for s in range(NQ):
            if s == SPLIT:
                two = [pieces[s], other]
                pl.when((shift == s) & (core == 0))(functools.partial(start, n, two))
                pl.when((shift == s) & (core == 1))(functools.partial(start, n, two[::-1]))
            else:
                piece = direct if (n, s) == (1, NQ - 1) else pieces[s]
                pl.when(shift == s)(functools.partial(start, n, sides(piece)))

    for n in range(2):
        for copy in copies(n, sides(pieces[0])):
            copy.wait()


def sort(pos, pieces):
    shape = jax.ShapeDtypeStruct((2 * CH * B, B), F32)
    return pl.pallas_call(
        sort_kernel,
        out_shape=[shape, shape],
        in_specs=[SM] + [ANY] * (NQ + 2),
        out_specs=[VM, VM],
        scratch_shapes=[pltpu.SemaphoreType.DMA((2, 2))],
        compiler_params=params(4),
        cost_estimate=cost(2),
        name="sort",
    )(pos, *pieces)


def panels_kernel(pos, inv, facing, keep, got, out, held, chunk, load, store):
    core = pos[1] % 2
    half = CH * B
    lower, upper = pl.ds(0, half), pl.ds(half, half)

    def copies(sources):
        for k, (ref, at) in enumerate(sources):
            yield pltpu.make_async_copy(ref.at[at], held.at[k], load.at[k])

    even = ((keep, lower), (got, lower), (keep, upper))
    odd = ((got, lower), (keep, lower), (got, upper))

    @pl.when(core == 0)
    def _():
        for copy in copies(even):
            copy.start()

    @pl.when(core == 1)
    def _():
        for copy in copies(odd):
            copy.start()

    waits = list(copies(even))
    waits[0].wait()
    n0 = dot_t(held[0], inv[0], HI).astype(BF16)
    chunk[:, :B] = n0
    waits[1].wait()
    n1 = dot_t(held[1] - dot_t(n0, facing[0]), inv[1], HI).astype(BF16)
    chunk[:, B : 2 * B] = n1
    waits[2].wait()
    rest = held[2] - dot_t(n0, facing[1]) - dot_t(n1, facing[2])
    chunk[:, 2 * B :] = dot_t(rest, inv[2], HI).astype(BF16)
    stores = [
        pltpu.make_async_copy(chunk, out.at[pl.ds(q * half, half)], store.at[q]) for q in range(NQ)
    ]
    for copy in stores:
        copy.start()
    for copy in stores:
        copy.wait()


def panels(pos, inv, facing, keep, got):
    return pl.pallas_call(
        panels_kernel,
        out_shape=jax.ShapeDtypeStruct((NQ * CH * B, STEPS * B), BF16),
        in_specs=[SM, VM, VM, ANY, ANY],
        out_specs=ANY,
        scratch_shapes=[
            pltpu.VMEM((STEPS, CH * B, B), F32),
            pltpu.VMEM((CH * B, STEPS * B), BF16),
            pltpu.SemaphoreType.DMA((STEPS,)),
            pltpu.SemaphoreType.DMA((NQ,)),
        ],
        compiler_params=params(6),
        cost_estimate=cost(4),
        name="panels",
    )(pos, inv, facing, keep, got)


def solve_kernel(pos, work, inv, chunk, out):
    del chunk
    col = pos[1]

    @pl.when(col >= STEPS)
    def _():
        out[...] = work[...]

    @pl.when(col < STEPS)
    def _():
        inverse = inv[jnp.minimum(col, STEPS - 1)]

        def solve(b, carry):
            at = pl.ds(pl.multiple_of(b * (ROWS // NR), 8), ROWS // NR)
            out[at] = dot_t(work[at], inverse, HI)
            return carry

        lax.fori_loop(0, NR, solve, 0)


def solve(pos, work, inv, chunk):
    return pl.pallas_call(
        solve_kernel,
        out_shape=jax.ShapeDtypeStruct((ROWS, B), F32),
        in_specs=[SM, VM, VM, ANY],
        out_specs=VM,
        compiler_params=params(12),
        cost_estimate=cost(20),
        name="solve",
    )(pos, work, inv, chunk)


def across_kernel(pos, face, inv, parts):
    col = pos[1]
    lane = lax.broadcasted_iota(jnp.int32, (B, STEPS * B), 1) // B
    across = jnp.where(lane < col, face[...].astype(F32), 0.0)
    parts[0] = across.astype(BF16)

    @pl.when(col < STEPS)
    def _():
        inverse = inv[jnp.minimum(col, STEPS - 1)]
        rest = lax.dot_general(
            inverse, across, (((1,), (0,)), ((), ())), precision=HI, preferred_element_type=F32
        )
        for i in range(3):
            parts[i] = rest.astype(BF16)
            rest = rest - parts[i].astype(F32)


def across(pos, face, inv):
    return pl.pallas_call(
        across_kernel,
        out_shape=jax.ShapeDtypeStruct((3, B, STEPS * B), BF16),
        in_specs=[SM, VM, VM],
        out_specs=VM,
        compiler_params=params(3),
        cost_estimate=cost(1),
        name="across",
    )(pos, face, inv)


def update_kernel(flip, pos, work, panel, parts, low, out, held, ins, outs):
    row, col = pos[0], pos[1]
    size = CH * B
    core = (col + flip) % 2

    def each(q, there, act):
        owner = 2 * q + core
        sems = outs if there else ins
        for n, (first, t, end) in enumerate(((owner, 0, 1), (TOP + 3 * owner, 1, CH))):
            hbm = pl.ds(pl.multiple_of(first * B, B), (end - t) * B)
            here = held.at[q, pl.ds(t * B, (end - t) * B)]
            copy = (
                pltpu.make_async_copy(here, out.at[hbm], sems.at[q, n])
                if there
                else pltpu.make_async_copy(work.at[hbm], here, sems.at[q, n])
            )
            if t and q == NQ - 1:
                pl.when(owner < NC - 1)(lambda copy=copy: act(copy))
            else:
                act(copy)

    for q in range(NQ):
        each(q, False, lambda copy: copy.start())
    for q in range(NQ):
        owner = 2 * q + core
        rows = slice(q * size, (q + 1) * size)
        each(q, False, lambda copy: copy.wait())

        @pl.when(col >= STEPS)
        def _(q=q, rows=rows):
            held[q] = held[q] - dot_t(panel[rows], parts[0])

        for k in range(1, STEPS):

            @pl.when(col == k)
            def _(k=k, q=q, rows=rows):
                left = panel[rows, : k * B]
                total = dot_t(left, parts[0, :, : k * B])
                for i in range(1, 3):
                    total = total + dot_t(left, parts[i, :, : k * B])
                held[q] = held[q] - total

        @pl.when((row == 0) & (owner <= col))
        def _(q=q, owner=owner):
            r = lax.broadcasted_iota(jnp.int32, (B, B), 0)
            c = lax.broadcasted_iota(jnp.int32, (B, B), 1)
            value = jnp.where(col < STEPS, low[jnp.minimum(col, STEPS - 1)], held[q, :B])
            held[q, :B] = jnp.where((owner == col) & (r >= c), value, 0.0)

        each(q, True, lambda copy: copy.start())

    for q in range(NQ):
        each(q, True, lambda copy: copy.wait())


def update(flip, pos, work, panel, parts, low):
    return pl.pallas_call(
        functools.partial(update_kernel, flip),
        out_shape=jax.ShapeDtypeStruct((ROWS, B), F32),
        in_specs=[SM, ANY, VM, VM, VM],
        out_specs=ANY,
        input_output_aliases={1: 0},
        scratch_shapes=[
            pltpu.VMEM((NQ, CH * B, B), F32),
            pltpu.SemaphoreType.DMA((NQ, 2)),
            pltpu.SemaphoreType.DMA((NQ, 2)),
        ],
        compiler_params=params(8),
        cost_estimate=cost(6),
        name="update",
    )(pos, work, panel, parts, low)


def send(x, pairs):
    return lax.ppermute(x, ("row", "col"), [(a * NC + b, c * NC + d) for (a, b), (c, d) in pairs])


def spread_top(front, row, col):
    part = front[: STEPS * B]
    a = send(part, [((0, 0), (0, 2)), ((0, 1), (0, 0)), ((0, 2), (0, 4))])
    b = send(part, [((0, 0), (0, 4)), ((0, 1), (0, 2)), ((0, 2), (0, 6))])
    c = send(part, [((0, 0), (0, 6)), ((0, 1), (0, 4)), ((0, 2), (0, 0))])
    d = send(part, [((0, 1), (0, 6))])

    def pick(at0, at2, at4, at6):
        return jnp.where(col == 0, at0, jnp.where(col == 2, at2, jnp.where(col == 4, at4, at6)))

    columns = [pick(part, a, b, c), pick(a, b, c, d), pick(c, part, a, b)]
    rooted = (row == 0) & (col < NC // 2) & (col % 2 == 0)
    top = jnp.concatenate([v[k * B :] for k, v in enumerate(columns)])
    top = jnp.where(rooted, top, 0.0)

    def hop(top, *moves):
        return sum([send(top, pairs) for pairs in moves], top)

    near = (0, 2, 4, 6)
    beside = [[((0, c), (dr, c + dc)) for c in near] for dr, dc in ((0, 8), (1, 0), (1, 8))]
    top = hop(top, *beside)
    even = range(0, NC, 2)
    away = [[((r, c), (r + dr, c)) for r in range(2) for c in even] for dr in (4, 2, 6)]
    top = hop(top, *away)
    return hop(top, [((r, c), (r, c + 1)) for c in even for r in range(NR)])


def on_device(front, child_update, child_rows):
    row, col = lax.axis_index("row"), lax.axis_index("col")
    pos = jnp.stack([row, col]).astype(jnp.int32)
    packed = pack(pos, child_rows, child_update)
    got = lax.all_to_all(packed, "row", 0, 0, tiled=True)
    top = spread_top(front, row, col)
    low, inv, facing = factor(top)
    work, *chunks = assemble(pos, child_rows, front, got)

    def home(k, dx, dy):
        return dx * 8 + (k // 2 + dy) % 4 * 2 + k % 2

    def step(v, start, end, ks=range(STEPS)):
        return lax.ppermute(v, "col", [(home(k, *start), home(k, *end)) for k in ks])

    pieces = {0: chunks[0]}
    pairs = [(k, home(k, 0, 3)) for k in range(2)] + [(2, home(2, 1, 3))]
    relayed = lax.ppermute(chunks[7], "col", pairs)
    other = step(chunks[NQ], (0, 0), (0, 1))
    for s in (4, 1, 5, 3, 6, 2):
        pieces[s] = step(chunks[s], (0, 0), (s // 4, s % 4))
    pieces[7] = step(relayed, (0, 3), (1, 3), range(2))
    other = step(other, (0, 1), (1, 1))
    keep, give = sort(pos, [pieces[s] for s in range(NQ)] + [other, relayed])
    flip = [(c, c ^ 1) for c in range(NC)]
    chunk = panels(pos, inv, facing, keep, lax.ppermute(give, "col", flip))
    cores = [[c for c in range(NC) if c % 2 == p] for p in range(2)]
    mine = lax.all_to_all(
        chunk, "col", 0, 0, axis_index_groups=cores, tiled=True
    )
    face = jnp.where(row == 0, chunk[:B], jnp.zeros_like(chunk[:B]))

    def hop(face, *moves):
        return sum([lax.ppermute(face, "row", pairs) for pairs in moves], face)

    face = hop(face, [(0, 2)], [(0, 6)])
    face = hop(face, [(2, 4)])
    face = hop(face, [(0, 1), (2, 3), (4, 5), (6, 7)])
    parts = across(pos, face, inv)
    work = solve(pos, work, inv, chunk)
    work = update(0, pos, work, mine, parts, low)
    other = lax.ppermute(mine, "col", flip)
    return update(1, pos, work, other, parts, low)


def solution(mesh):
    in_specs = (P("row", "col"), P("row", "col"), P())
    return jax.shard_map(
        on_device, mesh=mesh, in_specs=in_specs, out_specs=P("row", "col"), check_vma=False
    )
```
